32 devices in a mesh: sec: 2 (over y), gy: 4 (over z), gx: 4 (over x, core).
Axes of the slice: x: 2, y: 2, z: 4, core: 2. Of those that a mesh axis runs over, the one named last changes fastest.
Arguments:
- ocean: bfloat16 [32, 3, 1024, 1536], P(('sec', 'gy'), None, None, 'gx'), may hold values from -6 to 6
- level_weight: float32 [32], replicated, may hold values from 0.25 to 2.5
- velocity_start: float32 [2, 1024, 1536], P(None, ('sec', 'gy'), 'gx'), may hold values from -3 to 3
- wind_stress: float32 [2, 1024, 1536], P(None, ('sec', 'gy'), 'gx'), may hold values from -3 to 3
- thickness: float32 [1024, 1536], P(('sec', 'gy'), 'gx'), may hold values from 0.5 to 2.5
- concentration: float32 [1024, 1536], P(('sec', 'gy'), 'gx'), may hold values from 0.3 to 1
- ice_mask: int32 [1024, 1536], P(('sec', 'gy'), 'gx'), may hold values 0 or 1
- land_mask: int32 [1024, 1536], P(('sec', 'gy'), 'gx'), may hold values 0 or 1
Outputs:
- ice_velocity: float32 [2, 1024, 1536], P(None, ('sec', 'gy'), 'gx')
- ice_stress: float32 [3, 1024, 1536], P(None, ('sec', 'gy'), 'gx')
The draws below stay inside these ranges and needn't reach their ends.
All inputs are finite; a program needn't handle non-finite values. No bound on the sum of `ice_mask` or of `land_mask` on one device may be relied on, other than what follows from the above.
Results may differ from the reference program's by a relative error of at most 0.0003.
Values may be sent and summed in bfloat16 or wider, within the bound.
A program may use at most 128 MiB of HBM per device.

```python
import math
import jax
import jax.numpy as jnp
from jax import lax

SUB = 4
LEV = 32
NY = 1024
NX = 1536


def place_ends(array, rng, least, largest):
    dims = array.shape
    index_at = [jax.random.randint(jax.random.fold_in(rng, axis), (), 0, dims[axis]) for axis in range(len(dims))]
    array = array.at[tuple(index_at)].set(least)
    longest = dims.index(max(dims))
    index_at[longest] = (index_at[longest] + 1) % dims[longest]
    return array.at[tuple(index_at)].set(largest)


def with_spikes(result, rng, source, target, blocks, factor):
    def block_of(axis_at):
        return (jnp.arange(result.shape[axis_at]) // (result.shape[axis_at] // blocks)).reshape((-1,) + (1,) * (result.ndim - 1 - axis_at))

    first = jax.random.permutation(rng, blocks)[block_of(target)]
    far = (block_of(target) + blocks // 2) % blocks
    return jnp.where((block_of(source) == first) | (block_of(source) == far), factor * result, result)


def block_levels(key, dims, pieces, least, high):
    loudness = 1.0
    for axis_at, parts in pieces:
        heights = jax.random.uniform(jax.random.fold_in(jax.random.fold_in(key, 6), axis_at), (parts,), jnp.float32, least / len(pieces), high / len(pieces))
        loudness = loudness * jnp.repeat(jnp.exp(heights), dims[axis_at] // parts).reshape((-1,) + (1,) * (len(dims) - 1 - axis_at))
    return loudness


def normal_values(own_key, shape, scale, limit, shards=(), held_as=jnp.bfloat16):
    array = jax.random.normal(own_key, shape, jnp.float32) * scale
    if len(shards) > 0:
        array = block_levels(own_key, shape, shards, -0.22, 0.18) * array
    return jnp.clip(array, min=-limit, max=limit).astype(held_as)


def noise_with(rng, shape, deviation, most, cuts, heavy, held_as=jnp.bfloat16):
    drawn = deviation * jax.random.normal(rng, shape, jnp.float32)
    if cuts:
        drawn = drawn * block_levels(rng, shape, cuts, -0.22, 0.18)
    return jnp.clip(with_spikes(drawn, jax.random.fold_in(rng, 3), *heavy), -most, most).astype(held_as)


def setup_inputs(seed: int = 0) -> dict:
    arg_keys = jax.random.split(jax.random.key(seed), 9)
    ocean = noise_with(arg_keys[0], (LEV, 3, NY, NX), 1.0, 6.0, ((0, 8), (3, 4)), (0, 2, 8, 2.0))
    level_weight = jnp.clip(jnp.exp(jax.random.uniform(arg_keys[1], (LEV,), jnp.float32, math.log(0.25), math.log(2.5))), 0.25, 2.5)
    velocity_start = normal_values(arg_keys[2], (2, NY, NX), 0.5, 3.0, ((1, 8), (2, 4)), jnp.float32)
    wind_stress = normal_values(arg_keys[3], (2, NY, NX), 0.4, 3.0, ((1, 8), (2, 4)), jnp.float32)
    thickness = jnp.clip(0.5 + 2.0 * jax.random.uniform(arg_keys[4], (NY, NX), jnp.float32) ** block_levels(arg_keys[4], (NY, NX), ((0, 8), (1, 4)), -0.2, 0.2), 0.5, 2.5)
    concentration = jnp.clip(0.3 + 0.7 * jax.random.uniform(arg_keys[5], (NY, NX), jnp.float32) ** block_levels(arg_keys[5], (NY, NX), ((0, 8), (1, 4)), -0.2, 0.2), 0.3, 1.0)
    ice_mask = place_ends((jax.random.randint(arg_keys[6], (NY, NX), 0, 4) < 3).astype(jnp.int32), jax.random.fold_in(arg_keys[6], 1), 0, 1)
    land_mask = place_ends((jax.random.randint(arg_keys[7], (NY, NX), 0, 10) < 9).astype(jnp.int32), jax.random.fold_in(arg_keys[7], 1), 0, 1)
    return {"ocean": ocean, "level_weight": level_weight, "velocity_start": velocity_start, "wind_stress": wind_stress, "thickness": thickness, "concentration": concentration, "ice_mask": ice_mask, "land_mask": land_mask}


ecc_square = 4.0
strain_floor = 0.01
relax_rate = 0.5
water_drag = 0.8
coriolis_f = 0.5
slope_gain = 0.5
conc_decay = 4.0

def centre_x(field):
    return 0.5 * (field[..., 1:-1, 2:] - field[..., 1:-1, :-2])

def centre_y(field):
    return 0.5 * (field[..., 2:, 1:-1] - field[..., :-2, 1:-1])

def stresses(velocity, stress, strength, covered):
    east_u = centre_x(velocity[0])
    north_v = centre_y(velocity[1])
    north_u = centre_y(velocity[0])
    east_v = centre_x(velocity[1])
    spread = east_u + north_v
    tension = east_u - north_v
    shear = north_u + east_v
    delta = jnp.sqrt(spread * spread + (tension * tension + shear * shear) / ecc_square + strain_floor)
    first = (stress[0] + relax_rate * (strength * spread / delta - strength)) / (1.0 + relax_rate)
    second = (stress[1] + relax_rate * strength * tension / (ecc_square * delta)) / (1.0 + relax_rate)
    third = (stress[2] + relax_rate * strength * shear / (2.0 * ecc_square * delta)) / (1.0 + relax_rate)
    return jnp.stack([first, second, third]) * covered

def slope_force(height):
    return -slope_gain * jnp.stack([centre_x(height), centre_y(height)])

def momentum(velocity, stress, ice_mass, current, slope, wind_drag, moving):
    normal_x = 0.5 * (stress[0] + stress[1])
    normal_y = 0.5 * (stress[0] - stress[1])
    force_x = centre_x(normal_x) + centre_y(stress[2])
    force_y = centre_x(stress[2]) + centre_y(normal_y)
    rel_u = current[0] - velocity[0]
    rel_v = current[1] - velocity[1]
    drag = water_drag * jnp.sqrt(rel_u * rel_u + rel_v * rel_v)
    diagonal = ice_mass + drag
    turning = coriolis_f * ice_mass
    right_x = ice_mass * velocity[0] + force_x + drag * current[0] + wind_drag[0] + ice_mass * slope[0]
    right_y = ice_mass * velocity[1] + force_y + drag * current[1] + wind_drag[1] + ice_mass * slope[1]
    live = moving > 0.5
    denom = jnp.where(live, diagonal * diagonal + turning * turning, 1.0)
    new_u = jnp.where(live, (diagonal * right_x + turning * right_y) / denom, 0.0)
    new_v = jnp.where(live, (diagonal * right_y - turning * right_x) / denom, 0.0)
    return jnp.stack([new_u, new_v])

def extend(field, width):
    wide = jnp.concatenate([field[:, :, -width:], field, field[:, :, :width]], axis=2)
    return jnp.pad(wide, ((0, 0), (width, width), (0, 0)))

def reference(ocean, level_weight, velocity_start, wind_stress, thickness, concentration, ice_mask, land_mask):

    def add_level(level, total):
        return total + level_weight[level] * ocean[level].astype(jnp.float32)
    total = lax.fori_loop(0, LEV, add_level, jnp.zeros((3, NY, NX), jnp.float32))
    surface = total / math.sqrt(LEV)
    strength = jnp.exp(-conc_decay * (1.0 - concentration)) * thickness
    covered = ice_mask.astype(jnp.float32)
    moving = covered * land_mask.astype(jnp.float32)
    slope = slope_force(extend(surface[2:3], 1)[0])
    velocity = velocity_start
    stress = jnp.zeros((3, NY, NX), jnp.float32)
    for cycle in range(SUB):
        stress = stresses(extend(velocity, 1), stress, strength, covered)
        velocity = momentum(velocity, extend(stress, 1), thickness, surface[0:2], slope, wind_stress, moving)
    return (velocity, stress)
```

```python
import functools
import math

import jax
import jax.numpy as jnp
from jax import lax
from jax.experimental import pallas as pl
from jax.experimental.pallas import tpu as pltpu
from jax.sharding import PartitionSpec as P

SUB = 4
HALO = 8
LANES = 128
MESH = pl.DeviceIdType.MESH

U, V, WX, WY, THICK, STRENGTH, COVERED, MOVING = range(8)
FIELDS = 8


def kernel(
    dims,
    weight_ref,
    ocean_hbm,
    vel_hbm,
    wind_hbm,
    thick_hbm,
    conc_hbm,
    ice_hbm,
    land_hbm,
    vel_out,
    stress_out,
    ocean,
    total,
    y_send,
    y_recv,
    y_send_scale,
    y_recv_scale,
    z_send,
    z_recv,
    z_send_scale,
    z_recv_scale,
    own,
    masks,
    fields,
    stress,
    surf,
    ns_field,
    ew_field,
    ns_surf,
    ew_surf,
    ocean_sem,
    static_sem,
    y_sems,
    z_sems,
    ns_sems,
    ew_sems,
    out_sem,
):
    secs, rows_g, cols_g, levels = dims
    held = ocean_hbm.shape[0]
    tile_rows, tile_cols = thick_hbm.shape
    tiles = tile_cols // LANES
    top = 2 * HALO
    end = top + tile_rows
    s, g, x = lax.axis_index("sec"), lax.axis_index("gy"), lax.axis_index("gx")
    ranks = secs * rows_g
    rank = s * rows_g + g

    def at_rank(number):
        number = lax.rem(number + ranks, ranks)
        return (number // rows_g, lax.rem(number, rows_g), x)

    north, south = at_rank(rank - 1), at_rank(rank + 1)
    west = (s, g, lax.rem(x + cols_g - 1, cols_g))
    east = (s, g, lax.rem(x + 1, cols_g))
    over_secs = [(lax.rem(s + i, secs), g, x) for i in range(1, secs)]
    over_rows = [(s, lax.rem(g + k, rows_g), x) for k in range(1, rows_g)]

    order = [rows_g // 2] + [k for k in range(1, rows_g) if k != rows_g // 2] + [0]

    def block_rows(sec, k):
        block = sec * rows_g + lax.rem(g + k, rows_g)
        return pl.ds(pl.multiple_of(block * tile_rows, tile_rows), tile_rows)

    ocean_copies = {}
    for i in list(range(1, secs)) + [0]:
        for k in order:
            at = block_rows(lax.rem(s + i, secs), k)
            copy = pltpu.make_async_copy(
                ocean_hbm.at[:, :, at, :], ocean.at[i * rows_g + k], ocean_sem.at[i * rows_g + k]
            )
            copy.start()
            ocean_copies[i, k] = copy
    static_copies = []
    for j in range(tiles):
        cols = pl.ds(j * LANES, LANES)
        rows = pl.ds(top, tile_rows)
        for n, (source, target) in enumerate(
            (
                (vel_hbm.at[:, :, cols], fields.at[pl.ds(U, 2), j, rows, :]),
                (wind_hbm.at[:, :, cols], fields.at[pl.ds(WX, 2), j, rows, :]),
                (thick_hbm.at[:, cols], fields.at[THICK, j, rows, :]),
                (conc_hbm.at[:, cols], fields.at[STRENGTH, j, rows, :]),
                (ice_hbm.at[:, cols], masks.at[0, j]),
                (land_hbm.at[:, cols], masks.at[1, j]),
            )
        ):
            copy = pltpu.make_async_copy(source, target, static_sem.at[j, n])
            copy.start()
            static_copies.append(copy)

    barrier = pltpu.get_barrier_semaphore()
    partners = over_secs + over_rows + [north, south, west, east]
    for partner in partners:
        pl.semaphore_signal(barrier, inc=1, device_id=partner, device_id_type=MESH)
    pl.semaphore_wait(barrier, len(partners))

    def remote(source, target, sems, device):
        return pltpu.make_async_remote_copy(
            src_ref=source,
            dst_ref=target,
            send_sem=sems.at[0],
            recv_sem=sems.at[1],
            device_id=device,
            device_id_type=MESH,
        )

    own_weights = [weight_ref[rank * held + k] for k in range(held)]
    strips = tile_rows // 16

    def level_sum(slot, c, at, j):
        cols = pl.ds(j * LANES, LANES)
        value = own_weights[0] * ocean[slot, 0, c, at, cols].astype(jnp.float32)
        for k in range(1, held):
            value = value + own_weights[k] * ocean[slot, k, c, at, cols].astype(jnp.float32)
        return value

    def twice(value):
        return jnp.concatenate([value, value], axis=0)

    def coded(value_of, target, scale_ref):
        def first(i, most):
            at = pl.ds(pl.multiple_of(i * 16, 16), 16)
            for j in range(tiles):
                value = value_of(at, j)
                total[at, pl.ds(j * LANES, LANES)] = value
                most = jnp.maximum(most, jnp.abs(value))
            return most

        most = lax.fori_loop(0, strips, first, jnp.zeros((16, LANES), jnp.float32))
        most = jnp.maximum(jnp.maximum(most[0:8], most[8:16]), 1e-30)
        scale_ref[...] = most * (1.0 / 32767.0)
        inverse = twice(32767.0 / most)

        @pl.loop(0, strips)
        def _(i):
            at = pl.ds(pl.multiple_of(i * 16, 16), 16)
            for j in range(tiles):
                cols = pl.ds(j * LANES, LANES)
                code = jnp.round(total[at, cols] * inverse)
                target[at, cols] = code.astype(jnp.int32).astype(jnp.int16)

    def decoded(code_ref, scale, at, j):
        code = code_ref[at, pl.ds(j * LANES, LANES)].astype(jnp.int32)
        return code.astype(jnp.float32) * scale

    y_copies = {}
    for i in range(1, secs):
        for k in order:
            ocean_copies[i, k].wait()
            for c in range(3):
                slot = ((i - 1) * rows_g + k, c)
                coded(
                    lambda at, j, i=i, k=k, c=c: level_sum(i * rows_g + k, c, at, j),
                    y_send.at[slot],
                    y_send_scale.at[slot],
                )
                pair = (
                    remote(y_send.at[slot], y_recv.at[slot], y_sems.at[slot + (0,)], over_secs[i - 1]),
                    remote(
                        y_send_scale.at[slot],
                        y_recv_scale.at[slot],
                        y_sems.at[slot + (1,)],
                        over_secs[i - 1],
                    ),
                )
                for copy in pair:
                    copy.start()
                y_copies[i, k, c] = pair

    for copy in static_copies:
        copy.wait()

    @pl.loop(0, tile_rows // 8)
    def _(i):
        at = pl.ds(pl.multiple_of(i * 8, 8), 8)
        to = pl.ds(pl.multiple_of(i * 8 + top, 8), 8)
        for j in range(tiles):
            conc = fields[STRENGTH, j, to, :]
            fields[STRENGTH, j, to, :] = jnp.exp(-4.0 * (1.0 - conc)) * fields[THICK, j, to, :]
            ice = masks[0, j, at, :].astype(jnp.float32)
            fields[COVERED, j, to, :] = ice
            fields[MOVING, j, to, :] = ice * masks[1, j, at, :].astype(jnp.float32)

    inner = pl.ds(0, tiles)

    def send_rows(source, target, sems):
        up = remote(
            source.at[:, inner, pl.ds(top, HALO), :], target.at[1], sems.at[0], north
        )
        down = remote(
            source.at[:, inner, pl.ds(end - HALO, HALO), :], target.at[0], sems.at[1], south
        )
        up.start()
        down.start()
        return up, down

    def place_rows(target, received, count):
        above = jnp.where(rank > 0, 1.0, 0.0)
        below = jnp.where(rank < ranks - 1, 1.0, 0.0)
        for f in range(count):
            for j in range(tiles):
                target[f, j, pl.ds(HALO, HALO), :] = received[0, f, j] * above
                target[f, j, pl.ds(end, HALO), :] = received[1, f, j] * below

    full = pl.ds(HALO, tile_rows + 2 * HALO)

    def send_columns(source, target, sems):
        left = remote(source.at[:, 0, full, :], target.at[1], sems.at[0], west)
        right = remote(source.at[:, tiles - 1, full, :], target.at[0], sems.at[1], east)
        left.start()
        right.start()
        return left, right

    lane = lax.broadcasted_iota(jnp.int32, (8, LANES), 1)
    all_strips = (tile_rows + 2 * HALO) // 8

    def place_columns(target, received, count):
        @pl.loop(0, all_strips)
        def _(i):
            at = pl.ds(pl.multiple_of(i * 8, 8), 8)
            to = pl.ds(pl.multiple_of(i * 8 + HALO, 8), 8)
            for f in range(count):
                target[f, tiles, to, :] = jnp.where(
                    lane < HALO,
                    received[1, f, at, :],
                    jnp.where(lane >= LANES - HALO, received[0, f, at, :], 0.0),
                )

    field_rows = send_rows(fields, ns_field, ns_sems.at[0])

    z_copies = []
    field_columns = None
    for k in order:
        ocean_copies[0, k].wait()
        for c in range(3):
            slots = [((i - 1) * rows_g + k, c) for i in range(1, secs)]
            for i in range(1, secs):
                for copy in y_copies[i, k, c]:
                    copy.wait_recv()
            scales = [twice(y_recv_scale[slot]) for slot in slots]

            def value_of(at, j, k=k, c=c, slots=slots, scales=scales):
                value = level_sum(k, c, at, j)
                for slot, scale in zip(slots, scales):
                    value = value + decoded(y_recv.at[slot], scale, at, j)
                return value

            if k == 0:

                @pl.loop(0, strips)
                def _(i, value_of=value_of, c=c):
                    at = pl.ds(pl.multiple_of(i * 16, 16), 16)
                    for j in range(tiles):
                        own[c, at, pl.ds(j * LANES, LANES)] = value_of(at, j)
            else:
                slot = (k - 1, c)
                coded(value_of, z_send.at[slot], z_send_scale.at[slot])
                pair = (
                    remote(z_send.at[slot], z_recv.at[slot], z_sems.at[slot + (0,)], over_rows[k - 1]),
                    remote(
                        z_send_scale.at[slot],
                        z_recv_scale.at[slot],
                        z_sems.at[slot + (1,)],
                        over_rows[k - 1],
                    ),
                )
                for copy in pair:
                    copy.start()
                z_copies.append(pair)
        if k == order[0]:
            for copy in field_rows:
                copy.wait()
            place_rows(fields, ns_field, FIELDS)
            field_columns = send_columns(fields, ew_field, ew_sems.at[0])

    for copy in field_columns:
        copy.wait()
    place_columns(fields, ew_field, FIELDS)
    every = tiles + 1

    def margins(target, count):
        zero = jnp.zeros((8, LANES), jnp.float32)
        for f in range(count):
            for j in range(every):
                target[f, j, pl.ds(0, HALO), :] = zero
                target[f, j, pl.ds(end + HALO, HALO), :] = zero

    margins(fields, 2)
    margins(stress, 3)
    margins(surf, 3)

    def sides(values):
        before = [pltpu.roll(value, 1, 1) for value in values]
        after = [pltpu.roll(value, LANES - 1, 1) for value in values]
        out = []
        for j in range(every):
            low = jnp.where(lane == 0, before[j - 1], before[j])
            high = jnp.where(lane == LANES - 1, after[(j + 1) % every], after[j])
            out.append(0.5 * (high - low))
        return out

    def strip_rows(i, shift):
        if shift == 0:
            return pl.ds(pl.multiple_of(i * 8 + HALO, 8), 8)
        return pl.ds(i * 8 + HALO + shift, 8)

    def rows_of(ref, f, at):
        return [ref[f, j, at, :] for j in range(every)]

    def stress_step(first):
        @pl.loop(0, all_strips)
        def _(i):
            at, up, down = strip_rows(i, 0), strip_rows(i, -1), strip_rows(i, 1)
            east_u = sides(rows_of(fields, U, at))
            east_v = sides(rows_of(fields, V, at))
            for j in range(every):
                north_u = 0.5 * (fields[U, j, down, :] - fields[U, j, up, :])
                north_v = 0.5 * (fields[V, j, down, :] - fields[V, j, up, :])
                spread = east_u[j] + north_v
                tension = east_u[j] - north_v
                shear = north_u + east_v[j]
                turned = lax.rsqrt(
                    spread * spread + 0.25 * (tension * tension + shear * shear) + 0.01
                )
                half = 0.5 * fields[STRENGTH, j, at, :]
                rate = half * turned
                covered = fields[COVERED, j, at, :] * (1.0 / 1.5)
                new0 = rate * spread - half
                new1 = (0.25 * rate) * tension
                new2 = (0.125 * rate) * shear
                if not first:
                    new0 = stress[0, j, at, :] + new0
                    new1 = stress[1, j, at, :] + new1
                    new2 = stress[2, j, at, :] + new2
                stress[0, j, at, :] = new0 * covered
                stress[1, j, at, :] = new1 * covered
                stress[2, j, at, :] = new2 * covered

    def velocity_step():
        @pl.loop(0, all_strips)
        def _(i):
            at, up, down = strip_rows(i, 0), strip_rows(i, -1), strip_rows(i, 1)
            first = rows_of(stress, 0, at)
            second = rows_of(stress, 1, at)
            east_normal = sides([0.5 * (a + b) for a, b in zip(first, second)])
            east_third = sides(rows_of(stress, 2, at))
            for j in range(every):
                north_third = 0.5 * (stress[2, j, down, :] - stress[2, j, up, :])
                north_normal = 0.25 * (
                    (stress[0, j, down, :] - stress[1, j, down, :])
                    - (stress[0, j, up, :] - stress[1, j, up, :])
                )
                u, v = fields[U, j, at, :], fields[V, j, at, :]
                cx, cy = surf[0, j, at, :], surf[1, j, at, :]
                mass = fields[THICK, j, at, :]
                rel_u, rel_v = cx - u, cy - v
                drag = 0.8 * jnp.sqrt(rel_u * rel_u + rel_v * rel_v)
                a = mass + drag
                b = 0.5 * mass
                rx = mass * u + (east_normal[j] + north_third) + drag * cx + fields[WX, j, at, :]
                ry = mass * v + (east_third[j] + north_normal) + drag * cy + fields[WY, j, at, :]
                live = fields[MOVING, j, at, :] > 0.5
                inverse = 1.0 / jnp.where(live, a * a + b * b, 1.0)
                fields[U, j, at, :] = jnp.where(live, (a * rx + b * ry) * inverse, 0.0)
                fields[V, j, at, :] = jnp.where(live, (a * ry - b * rx) * inverse, 0.0)

    stress_step(True)

    for pair in z_copies:
        for copy in pair:
            copy.wait_recv()
    norm = 1.0 / math.sqrt(levels)
    for c in range(3):
        scales = [twice(z_recv_scale[k, c]) for k in range(rows_g - 1)]

        @pl.loop(0, strips)
        def _(i, c=c, scales=scales):
            at = pl.ds(pl.multiple_of(i * 16, 16), 16)
            to = pl.ds(pl.multiple_of(i * 16 + top, 8), 16)
            for j in range(tiles):
                value = own[c, at, pl.ds(j * LANES, LANES)]
                for k in range(rows_g - 1):
                    value = value + decoded(z_recv.at[k, c], scales[k], at, j)
                surf[c, j, to, :] = value * norm

    for copy in send_rows(surf, ns_surf, ns_sems.at[1]):
        copy.wait()
    place_rows(surf, ns_surf, 3)
    for copy in send_columns(surf, ew_surf, ew_sems.at[1]):
        copy.wait()
    place_columns(surf, ew_surf, 3)

    @pl.loop(0, all_strips)
    def _(i):
        at, up, down = strip_rows(i, 0), strip_rows(i, -1), strip_rows(i, 1)
        slope_x = sides(rows_of(surf, 2, at))
        for j in range(every):
            slope_y = 0.5 * (surf[2, j, down, :] - surf[2, j, up, :])
            gain = -0.5 * fields[THICK, j, at, :]
            fields[WX, j, at, :] = fields[WX, j, at, :] + gain * slope_x[j]
            fields[WY, j, at, :] = fields[WY, j, at, :] + gain * slope_y

    velocity_step()

    @pl.loop(0, SUB - 2)
    def _(cycle):
        stress_step(False)
        velocity_step()

    stress_step(False)
    outs = []
    rows = pl.ds(top, tile_rows)
    for j in range(tiles):
        copy = pltpu.make_async_copy(
            stress.at[:, j, rows, :], stress_out.at[:, :, pl.ds(j * LANES, LANES)], out_sem.at[0, j]
        )
        copy.start()
        outs.append(copy)
    velocity_step()
    for j in range(tiles):
        copy = pltpu.make_async_copy(
            fields.at[pl.ds(U, 2), j, rows, :],
            vel_out.at[:, :, pl.ds(j * LANES, LANES)],
            out_sem.at[1, j],
        )
        copy.start()
        outs.append(copy)
    for copy in outs:
        copy.wait()
    for pair in list(y_copies.values()) + z_copies:
        for copy in pair:
            copy.wait_send()


def body(
    ocean, level_weight, velocity_start, wind_stress, thickness, concentration, ice_mask, land_mask
):
    secs, rows_g, cols_g = lax.axis_size("sec"), lax.axis_size("gy"), lax.axis_size("gx")
    held = ocean.shape[0]
    rows, cols = thickness.shape
    tiles = cols // LANES
    tall = rows + 4 * HALO
    wide_rows = rows + 2 * HALO
    f32, i16 = jnp.float32, jnp.int16
    dma = pltpu.SemaphoreType.DMA
    y_slots = (secs - 1) * rows_g
    z_slots = rows_g - 1
    anywhere = pl.BlockSpec(memory_space=pl.ANY)
    return pl.pallas_call(
        functools.partial(kernel, (secs, rows_g, cols_g, level_weight.shape[0])),
        out_shape=(
            jax.ShapeDtypeStruct((2, rows, cols), f32),
            jax.ShapeDtypeStruct((3, rows, cols), f32),
        ),
        in_specs=[pl.BlockSpec(memory_space=pltpu.SMEM)] + [anywhere] * 7,
        out_specs=(anywhere, anywhere),
        scratch_shapes=[
            pltpu.VMEM((secs * rows_g, held, 3, rows, cols), ocean.dtype),
            pltpu.VMEM((rows, cols), f32),
            pltpu.VMEM((y_slots, 3, rows, cols), i16),
            pltpu.VMEM((y_slots, 3, rows, cols), i16),
            pltpu.VMEM((y_slots, 3, 8, LANES), f32),
            pltpu.VMEM((y_slots, 3, 8, LANES), f32),
            pltpu.VMEM((z_slots, 3, rows, cols), i16),
            pltpu.VMEM((z_slots, 3, rows, cols), i16),
            pltpu.VMEM((z_slots, 3, 8, LANES), f32),
            pltpu.VMEM((z_slots, 3, 8, LANES), f32),
            pltpu.VMEM((3, rows, cols), f32),
            pltpu.VMEM((2, tiles, rows, LANES), jnp.int32),
            pltpu.VMEM((FIELDS, tiles + 1, tall, LANES), f32),
            pltpu.VMEM((3, tiles + 1, tall, LANES), f32),
            pltpu.VMEM((3, tiles + 1, tall, LANES), f32),
            pltpu.VMEM((2, FIELDS, tiles, HALO, LANES), f32),
            pltpu.VMEM((2, FIELDS, wide_rows, LANES), f32),
            pltpu.VMEM((2, 3, tiles, HALO, LANES), f32),
            pltpu.VMEM((2, 3, wide_rows, LANES), f32),
            dma((secs * rows_g,)),
            dma((tiles, 6)),
            dma((y_slots, 3, 2, 2)),
            dma((z_slots, 3, 2, 2)),
            dma((2, 2, 2)),
            dma((2, 2, 2)),
            dma((2, tiles)),
        ],
        compiler_params=pltpu.CompilerParams(
            collective_id=0, has_side_effects=True, vmem_limit_bytes=60 * 1024 * 1024
        ),
    )(
        level_weight,
        ocean,
        velocity_start,
        wind_stress,
        thickness,
        concentration,
        ice_mask,
        land_mask,
    )


def solution(mesh):
    placed = (
        P(("sec", "gy"), None, None, "gx"),
        P(),
        P(None, ("sec", "gy"), "gx"),
        P(None, ("sec", "gy"), "gx"),
        P(("sec", "gy"), "gx"),
        P(("sec", "gy"), "gx"),
        P(("sec", "gy"), "gx"),
        P(("sec", "gy"), "gx"),
    )
    return jax.shard_map(
        body,
        mesh=mesh,
        in_specs=placed,
        out_specs=(P(None, ("sec", "gy"), "gx"), P(None, ("sec", "gy"), "gx")),
        check_vma=False,
    )
```

```python
import functools
import math

import jax
import jax.numpy as jnp
from jax import lax
from jax.experimental import pallas as pl
from jax.experimental.pallas import tpu as pltpu
from jax.sharding import PartitionSpec as P

SUB = 4
HALO = 8
VMEM_OUT = 8 * 1024 * 1024
LANES = 128
MESH = pl.DeviceIdType.MESH

U, V, WX, WY, THICK, STRENGTH, COVERED, MOVING = range(8)
FIELDS = 8


def kernel(
    dims,
    weight_ref,
    ocean_hbm,
    vel_hbm,
    wind_hbm,
    thick_hbm,
    conc_hbm,
    ice_hbm,
    land_hbm,
    fields,
    stress,
    ocean,
    total,
    y_send,
    y_recv,
    y_send_scale,
    y_recv_scale,
    z_send,
    z_recv,
    z_send_scale,
    z_recv_scale,
    own,
    masks,
    surf,
    ns_field,
    ew_field,
    ns_surf,
    side_send,
    side_recv,
    corner_recv,
    ocean_sem,
    static_sem,
    y_sems,
    z_sems,
    ns_sems,
    ew_sems,
    surf_sems,
):
    secs, rows_g, cols_g, levels = dims
    held = ocean_hbm.shape[0]
    tile_rows, tile_cols = thick_hbm.shape
    tiles = tile_cols // LANES
    top = 2 * HALO
    end = top + tile_rows
    s, g, x = lax.axis_index("sec"), lax.axis_index("gy"), lax.axis_index("gx")
    ranks = secs * rows_g
    rank = s * rows_g + g

    def at_rank(number):
        number = lax.rem(number + ranks, ranks)
        return (number // rows_g, lax.rem(number, rows_g), x)

    north, south = at_rank(rank - 1), at_rank(rank + 1)
    west = (s, g, lax.rem(x + cols_g - 1, cols_g))
    east = (s, g, lax.rem(x + 1, cols_g))
    north_west, north_east = north[:2] + west[2:], north[:2] + east[2:]
    south_west, south_east = south[:2] + west[2:], south[:2] + east[2:]
    over_secs = [(lax.rem(s + i, secs), g, x) for i in range(1, secs)]
    over_rows = [(s, lax.rem(g + k, rows_g), x) for k in range(1, rows_g)]

    order = [rows_g // 2] + [k for k in range(1, rows_g) if k != rows_g // 2] + [0]

    def block_rows(sec, k):
        block = sec * rows_g + lax.rem(g + k, rows_g)
        return pl.ds(pl.multiple_of(block * tile_rows, tile_rows), tile_rows)

    ocean_copies = {}
    for i in list(range(1, secs)) + [0]:
        for k in order:
            at = block_rows(lax.rem(s + i, secs), k)
            copy = pltpu.make_async_copy(
                ocean_hbm.at[:, :, at, :], ocean.at[i * rows_g + k], ocean_sem.at[i * rows_g + k]
            )
            copy.start()
            ocean_copies[i, k] = copy
    static_copies = []
    for j in range(tiles):
        cols = pl.ds(j * LANES, LANES)
        rows = pl.ds(top, tile_rows)
        for n, (source, target) in enumerate(
            (
                (vel_hbm.at[:, :, cols], fields.at[pl.ds(U, 2), j, rows, :]),
                (wind_hbm.at[:, :, cols], fields.at[pl.ds(WX, 2), j, rows, :]),
                (thick_hbm.at[:, cols], fields.at[THICK, j, rows, :]),
                (conc_hbm.at[:, cols], fields.at[STRENGTH, j, rows, :]),
                (ice_hbm.at[:, cols], masks.at[0, j]),
                (land_hbm.at[:, cols], masks.at[1, j]),
            )
        ):
            copy = pltpu.make_async_copy(source, target, static_sem.at[j, n])
            copy.start()
            static_copies.append(copy)

    barrier = pltpu.get_barrier_semaphore()
    partners = over_secs + over_rows + [north, south, west, east]
    partners += [north_west, north_east, south_west, south_east]
    for partner in partners:
        pl.semaphore_signal(barrier, inc=1, device_id=partner, device_id_type=MESH)
    pl.semaphore_wait(barrier, len(partners))

    def remote(source, target, sems, device):
        return pltpu.make_async_remote_copy(
            src_ref=source,
            dst_ref=target,
            send_sem=sems.at[0],
            recv_sem=sems.at[1],
            device_id=device,
            device_id_type=MESH,
        )

    own_weights = [weight_ref[rank * held + k] for k in range(held)]
    strips = tile_rows // 16

    def level_sum(slot, c, at, j):
        cols = pl.ds(j * LANES, LANES)
        value = own_weights[0] * ocean[slot, 0, c, at, cols].astype(jnp.float32)
        for k in range(1, held):
            value = value + own_weights[k] * ocean[slot, k, c, at, cols].astype(jnp.float32)
        return value

    def twice(value):
        return jnp.concatenate([value, value], axis=0)

    def coded(value_of, target, scale_ref):
        def first(i, most):
            at = pl.ds(pl.multiple_of(i * 16, 16), 16)
            for j in range(tiles):
                value = value_of(at, j)
                total[at, pl.ds(j * LANES, LANES)] = value
                most = jnp.maximum(most, jnp.abs(value))
            return most

        most = lax.fori_loop(
            0, strips, first, jnp.zeros((16, LANES), jnp.float32), unroll=True
        )
        most = jnp.maximum(jnp.maximum(most[0:8], most[8:16]), 1e-30)
        scale_ref[...] = most * (1.0 / 32767.0)
        inverse = twice(32767.0 / most)

        @pl.loop(0, strips, unroll=True)
        def _(i):
            at = pl.ds(pl.multiple_of(i * 16, 16), 16)
            for j in range(tiles):
                cols = pl.ds(j * LANES, LANES)
                code = jnp.round(total[at, cols] * inverse)
                target[at, cols] = code.astype(jnp.int32).astype(jnp.int16)

    def decoded(code_ref, scale, at, j):
        code = code_ref[at, pl.ds(j * LANES, LANES)].astype(jnp.int32)
        return code.astype(jnp.float32) * scale

    y_copies = {}
    for i in range(1, secs):
        for k in order:
            ocean_copies[i, k].wait()
            for c in range(3):
                slot = ((i - 1) * rows_g + k, c)
                coded(
                    lambda at, j, i=i, k=k, c=c: level_sum(i * rows_g + k, c, at, j),
                    y_send.at[slot],
                    y_send_scale.at[slot],
                )
                pair = (
                    remote(y_send.at[slot], y_recv.at[slot], y_sems.at[slot + (0,)], over_secs[i - 1]),
                    remote(
                        y_send_scale.at[slot],
                        y_recv_scale.at[slot],
                        y_sems.at[slot + (1,)],
                        over_secs[i - 1],
                    ),
                )
                for copy in pair:
                    copy.start()
                y_copies[i, k, c] = pair

    for copy in static_copies:
        copy.wait()

    @pl.loop(0, tile_rows // 8)
    def _(i):
        at = pl.ds(pl.multiple_of(i * 8, 8), 8)
        to = pl.ds(pl.multiple_of(i * 8 + top, 8), 8)
        for j in range(tiles):
            conc = fields[STRENGTH, j, to, :]
            fields[STRENGTH, j, to, :] = jnp.exp(-4.0 * (1.0 - conc)) * fields[THICK, j, to, :]
            ice = masks[0, j, at, :].astype(jnp.float32)
            fields[COVERED, j, to, :] = ice
            fields[MOVING, j, to, :] = ice * masks[1, j, at, :].astype(jnp.float32)

    inner = pl.ds(0, tiles)

    def send_rows(source, target, sems):
        up = remote(
            source.at[:, inner, pl.ds(top, HALO), :], target.at[1], sems.at[0], north
        )
        down = remote(
            source.at[:, inner, pl.ds(end - HALO, HALO), :], target.at[0], sems.at[1], south
        )
        up.start()
        down.start()
        return up, down

    def place_rows(target, received, count):
        above = jnp.where(rank > 0, 1.0, 0.0)
        below = jnp.where(rank < ranks - 1, 1.0, 0.0)
        for f in range(count):
            for j in range(tiles):
                target[f, j, pl.ds(HALO, HALO), :] = received[0, f, j] * above
                target[f, j, pl.ds(end, HALO), :] = received[1, f, j] * below

    full = pl.ds(HALO, tile_rows + 2 * HALO)

    def send_columns(source, target, sems):
        left = remote(source.at[:, 0, full, :], target.at[1], sems.at[0], west)
        right = remote(source.at[:, tiles - 1, full, :], target.at[0], sems.at[1], east)
        left.start()
        right.start()
        return left, right

    lane = lax.broadcasted_iota(jnp.int32, (8, LANES), 1)
    all_strips = (tile_rows + 2 * HALO) // 8

    def place_columns(target, received, count):
        @pl.loop(0, all_strips)
        def _(i):
            at = pl.ds(pl.multiple_of(i * 8, 8), 8)
            to = pl.ds(pl.multiple_of(i * 8 + HALO, 8), 8)
            for f in range(count):
                target[f, tiles, to, :] = jnp.where(
                    lane < HALO,
                    received[1, f, at, :],
                    jnp.where(lane >= LANES - HALO, received[0, f, at, :], 0.0),
                )

    field_rows = send_rows(fields, ns_field, ns_sems)

    z_copies = []
    field_columns = None
    for k in order:
        ocean_copies[0, k].wait()
        for c in range(3):
            slots = [((i - 1) * rows_g + k, c) for i in range(1, secs)]
            for i in range(1, secs):
                for copy in y_copies[i, k, c]:
                    copy.wait_recv()
            scales = [twice(y_recv_scale[slot]) for slot in slots]

            def value_of(at, j, k=k, c=c, slots=slots, scales=scales):
                value = level_sum(k, c, at, j)
                for slot, scale in zip(slots, scales):
                    value = value + decoded(y_recv.at[slot], scale, at, j)
                return value

            if k == 0:

                @pl.loop(0, strips, unroll=True)
                def _(i, value_of=value_of, c=c):
                    at = pl.ds(pl.multiple_of(i * 16, 16), 16)
                    for j in range(tiles):
                        own[c, at, pl.ds(j * LANES, LANES)] = value_of(at, j)
            else:
                slot = (k - 1, c)
                coded(value_of, z_send.at[slot], z_send_scale.at[slot])
                pair = (
                    remote(z_send.at[slot], z_recv.at[slot], z_sems.at[slot + (0,)], over_rows[k - 1]),
                    remote(
                        z_send_scale.at[slot],
                        z_recv_scale.at[slot],
                        z_sems.at[slot + (1,)],
                        over_rows[k - 1],
                    ),
                )
                for copy in pair:
                    copy.start()
                z_copies.append(pair)
        if k == order[0]:
            for copy in field_rows:
                copy.wait()
            place_rows(fields, ns_field, FIELDS)
            field_columns = send_columns(fields, ew_field, ew_sems)

    for copy in field_columns:
        copy.wait()
    place_columns(fields, ew_field, FIELDS)
    every = tiles + 1

    def margins(target, count):
        zero = jnp.zeros((8, LANES), jnp.float32)
        for f in range(count):
            for j in range(every):
                target[f, j, pl.ds(0, HALO), :] = zero
                target[f, j, pl.ds(end + HALO, HALO), :] = zero

    margins(fields, 2)
    margins(stress, 3)
    margins(surf, 3)

    def sides(values):
        before = [pltpu.roll(value, 1, 1) for value in values]
        after = [pltpu.roll(value, LANES - 1, 1) for value in values]
        out = []
        for j in range(every):
            low = jnp.where(lane == 0, before[j - 1], before[j])
            high = jnp.where(lane == LANES - 1, after[(j + 1) % every], after[j])
            out.append(0.5 * (high - low))
        return out

    def strip_rows(i, shift):
        if shift == 0:
            return pl.ds(pl.multiple_of(i * 8 + HALO, 8), 8)
        return pl.ds(i * 8 + HALO + shift, 8)

    def rows_of(ref, f, at):
        return [ref[f, j, at, :] for j in range(every)]

    def stress_step(first):
        @pl.loop(0, all_strips, unroll=6)
        def _(i):
            at, up, down = strip_rows(i, 0), strip_rows(i, -1), strip_rows(i, 1)
            east_u = sides(rows_of(fields, U, at))
            east_v = sides(rows_of(fields, V, at))
            for j in range(every):
                north_u = 0.5 * (fields[U, j, down, :] - fields[U, j, up, :])
                north_v = 0.5 * (fields[V, j, down, :] - fields[V, j, up, :])
                spread = east_u[j] + north_v
                tension = east_u[j] - north_v
                shear = north_u + east_v[j]
                turned = lax.rsqrt(
                    spread * spread + 0.25 * (tension * tension + shear * shear) + 0.01
                )
                half = 0.5 * fields[STRENGTH, j, at, :]
                rate = half * turned
                covered = fields[COVERED, j, at, :] * (1.0 / 1.5)
                new0 = rate * spread - half
                new1 = (0.25 * rate) * tension
                new2 = (0.125 * rate) * shear
                if not first:
                    new0 = stress[0, j, at, :] + new0
                    new1 = stress[1, j, at, :] + new1
                    new2 = stress[2, j, at, :] + new2
                stress[0, j, at, :] = new0 * covered
                stress[1, j, at, :] = new1 * covered
                stress[2, j, at, :] = new2 * covered

    def velocity_step():
        @pl.loop(0, all_strips, unroll=6)
        def _(i):
            at, up, down = strip_rows(i, 0), strip_rows(i, -1), strip_rows(i, 1)
            first = rows_of(stress, 0, at)
            second = rows_of(stress, 1, at)
            east_normal = sides([0.5 * (a + b) for a, b in zip(first, second)])
            east_third = sides(rows_of(stress, 2, at))
            for j in range(every):
                north_third = 0.5 * (stress[2, j, down, :] - stress[2, j, up, :])
                north_normal = 0.25 * (
                    (stress[0, j, down, :] - stress[1, j, down, :])
                    - (stress[0, j, up, :] - stress[1, j, up, :])
                )
                u, v = fields[U, j, at, :], fields[V, j, at, :]
                cx, cy = surf[0, j, at, :], surf[1, j, at, :]
                mass = fields[THICK, j, at, :]
                rel_u, rel_v = cx - u, cy - v
                drag = 0.8 * jnp.sqrt(rel_u * rel_u + rel_v * rel_v)
                a = mass + drag
                b = 0.5 * mass
                rx = mass * u + (east_normal[j] + north_third) + drag * cx + fields[WX, j, at, :]
                ry = mass * v + (east_third[j] + north_normal) + drag * cy + fields[WY, j, at, :]
                live = fields[MOVING, j, at, :] > 0.5
                inverse = 1.0 / jnp.where(live, a * a + b * b, 1.0)
                fields[U, j, at, :] = jnp.where(live, (a * rx + b * ry) * inverse, 0.0)
                fields[V, j, at, :] = jnp.where(live, (a * ry - b * rx) * inverse, 0.0)

    stress_step(True)

    norm = 1.0 / math.sqrt(levels)
    tile_strips = tile_rows // 8
    per_piece = LANES // HALO
    halo_copies = []
    for c in range(3):
        for k in range(rows_g - 1):
            for copy in z_copies[k * 3 + c]:
                copy.wait_recv()
        scales = [twice(z_recv_scale[k, c]) for k in range(rows_g - 1)]

        @pl.loop(0, strips, unroll=True)
        def _(i, c=c, scales=scales):
            at = pl.ds(pl.multiple_of(i * 16, 16), 16)
            to = pl.ds(pl.multiple_of(i * 16 + top, 8), 16)
            for j in range(tiles):
                value = own[c, at, pl.ds(j * LANES, LANES)]
                for k in range(rows_g - 1):
                    value = value + decoded(z_recv.at[k, c], scales[k], at, j)
                surf[c, j, to, :] = value * norm

        for side, j, offset in ((0, 0, 0), (1, tiles - 1, HALO)):
            for piece in range(-(-tile_strips // per_piece)):
                packed = jnp.zeros((8, LANES), jnp.float32)
                for q in range(min(per_piece, tile_strips - piece * per_piece)):
                    value = surf[c, j, pl.ds(top + 8 * (piece * per_piece + q), 8), :]
                    shift = (q * HALO + offset) % LANES
                    value = pltpu.roll(value, shift, 1) if shift else value
                    packed = jnp.where(lane // HALO == q, value, packed)
                side_send[c, side, piece] = packed
        first, last = pl.ds(top, HALO), pl.ds(end - HALO, HALO)
        copies = []
        for n, (source, target, device) in enumerate(
            (
                (surf.at[c, inner, first, :], ns_surf.at[1, c], north),
                (surf.at[c, inner, last, :], ns_surf.at[0, c], south),
                (side_send.at[c, 0], side_recv.at[c, 1], west),
                (side_send.at[c, 1], side_recv.at[c, 0], east),
                (surf.at[c, 0, first, :], corner_recv.at[c, 3], north_west),
                (surf.at[c, tiles - 1, first, :], corner_recv.at[c, 2], north_east),
                (surf.at[c, 0, last, :], corner_recv.at[c, 1], south_west),
                (surf.at[c, tiles - 1, last, :], corner_recv.at[c, 0], south_east),
            )
        ):
            copy = remote(source, target, surf_sems.at[c, n], device)
            copy.start()
            copies.append(copy)
        halo_copies.append(copies)

    above = jnp.where(rank > 0, 1.0, 0.0)
    below = jnp.where(rank < ranks - 1, 1.0, 0.0)
    for c in range(3):
        for copy in halo_copies[c]:
            copy.wait()
        for j in range(tiles):
            surf[c, j, pl.ds(HALO, HALO), :] = ns_surf[0, c, j] * above
            surf[c, j, pl.ds(end, HALO), :] = ns_surf[1, c, j] * below

        def beyond(west_value, east_value):
            return jnp.where(
                lane < HALO, east_value, jnp.where(lane >= LANES - HALO, west_value, 0.0)
            )

        surf[c, tiles, pl.ds(HALO, HALO), :] = above * beyond(corner_recv[c, 0], corner_recv[c, 1])
        surf[c, tiles, pl.ds(end, HALO), :] = below * beyond(corner_recv[c, 2], corner_recv[c, 3])
        for t in range(tile_strips):
            piece, q = divmod(t, per_piece)
            from_west = side_recv[c, 0, piece]
            from_east = side_recv[c, 1, piece]
            back = (LANES - HALO - q * HALO) % LANES
            from_west = pltpu.roll(from_west, back, 1) if back else from_west
            back = (LANES - q * HALO) % LANES
            from_east = pltpu.roll(from_east, back, 1) if back else from_east
            surf[c, tiles, pl.ds(top + 8 * t, 8), :] = beyond(from_west, from_east)

    @pl.loop(0, all_strips, unroll=6)
    def _(i):
        at, up, down = strip_rows(i, 0), strip_rows(i, -1), strip_rows(i, 1)
        slope_x = sides(rows_of(surf, 2, at))
        for j in range(every):
            slope_y = 0.5 * (surf[2, j, down, :] - surf[2, j, up, :])
            gain = -0.5 * fields[THICK, j, at, :]
            fields[WX, j, at, :] = fields[WX, j, at, :] + gain * slope_x[j]
            fields[WY, j, at, :] = fields[WY, j, at, :] + gain * slope_y

    velocity_step()

    @pl.loop(0, SUB - 2)
    def _(cycle):
        stress_step(False)
        velocity_step()

    stress_step(False)
    velocity_step()
    for pair in list(y_copies.values()) + z_copies:
        for copy in pair:
            copy.wait_send()


def write_out(fields, stress, vel_out, stress_out, sems):
    tiles = fields.shape[1] - 1
    rows = pl.ds(2 * HALO, vel_out.shape[1])
    copies = []
    for j in range(tiles):
        cols = pl.ds(j * LANES, LANES)
        for n, (source, target) in enumerate(
            ((fields.at[pl.ds(U, 2)], vel_out), (stress, stress_out))
        ):
            copy = pltpu.make_async_copy(
                source.at[:, j, rows, :], target.at[:, :, cols], sems.at[n, j]
            )
            copy.start()
            copies.append(copy)
    for copy in copies:
        copy.wait()


def body(
    ocean, level_weight, velocity_start, wind_stress, thickness, concentration, ice_mask, land_mask
):
    secs, rows_g, cols_g = lax.axis_size("sec"), lax.axis_size("gy"), lax.axis_size("gx")
    held = ocean.shape[0]
    rows, cols = thickness.shape
    tiles = cols // LANES
    tall = rows + 4 * HALO
    wide_rows = rows + 2 * HALO
    pieces = pl.cdiv(rows, LANES)
    f32, i16 = jnp.float32, jnp.int16
    dma = pltpu.SemaphoreType.DMA
    y_slots = (secs - 1) * rows_g
    z_slots = rows_g - 1
    anywhere = pl.BlockSpec(memory_space=pl.ANY)
    on_chip = pl.BlockSpec(memory_space=pltpu.VMEM)
    fields, stress = pl.pallas_call(
        functools.partial(kernel, (secs, rows_g, cols_g, level_weight.shape[0])),
        out_shape=(
            pltpu.VMEM((FIELDS, tiles + 1, tall, LANES), f32),
            pltpu.VMEM((3, tiles + 1, tall, LANES), f32),
        ),
        in_specs=[pl.BlockSpec(memory_space=pltpu.SMEM)] + [anywhere] * 7,
        out_specs=(on_chip, on_chip),
        scratch_shapes=[
            pltpu.VMEM((secs * rows_g, held, 3, rows, cols), ocean.dtype),
            pltpu.VMEM((rows, cols), f32),
            pltpu.VMEM((y_slots, 3, rows, cols), i16),
            pltpu.VMEM((y_slots, 3, rows, cols), i16),
            pltpu.VMEM((y_slots, 3, 8, LANES), f32),
            pltpu.VMEM((y_slots, 3, 8, LANES), f32),
            pltpu.VMEM((z_slots, 3, rows, cols), i16),
            pltpu.VMEM((z_slots, 3, rows, cols), i16),
            pltpu.VMEM((z_slots, 3, 8, LANES), f32),
            pltpu.VMEM((z_slots, 3, 8, LANES), f32),
            pltpu.VMEM((3, rows, cols), f32),
            pltpu.VMEM((2, tiles, rows, LANES), jnp.int32),
            pltpu.VMEM((3, tiles + 1, tall, LANES), f32),
            pltpu.VMEM((2, FIELDS, tiles, HALO, LANES), f32),
            pltpu.VMEM((2, FIELDS, wide_rows, LANES), f32),
            pltpu.VMEM((2, 3, tiles, HALO, LANES), f32),
            pltpu.VMEM((3, 2, pieces, 8, LANES), f32),
            pltpu.VMEM((3, 2, pieces, 8, LANES), f32),
            pltpu.VMEM((3, 4, HALO, LANES), f32),
            dma((secs * rows_g,)),
            dma((tiles, 6)),
            dma((y_slots, 3, 2, 2)),
            dma((z_slots, 3, 2, 2)),
            dma((2, 2)),
            dma((2, 2)),
            dma((3, 8, 2)),
        ],
        compiler_params=pltpu.CompilerParams(
            collective_id=0, has_side_effects=True, vmem_limit_bytes=52 * 1024 * 1024
        ),
    )(
        level_weight,
        ocean,
        velocity_start,
        wind_stress,
        thickness,
        concentration,
        ice_mask,
        land_mask,
    )
    return pl.pallas_call(
        write_out,
        out_shape=(
            jax.ShapeDtypeStruct((2, rows, cols), f32),
            jax.ShapeDtypeStruct((3, rows, cols), f32),
        ),
        in_specs=[on_chip, on_chip],
        out_specs=(anywhere, anywhere),
        scratch_shapes=[dma((2, tiles))],
        compiler_params=pltpu.CompilerParams(vmem_limit_bytes=VMEM_OUT),
    )(fields, stress)


def solution(mesh):
    placed = (
        P(("sec", "gy"), None, None, "gx"),
        P(),
        P(None, ("sec", "gy"), "gx"),
        P(None, ("sec", "gy"), "gx"),
        P(("sec", "gy"), "gx"),
        P(("sec", "gy"), "gx"),
        P(("sec", "gy"), "gx"),
        P(("sec", "gy"), "gx"),
    )
    return jax.shard_map(
        body,
        mesh=mesh,
        in_specs=placed,
        out_specs=(P(None, ("sec", "gy"), "gx"), P(None, ("sec", "gy"), "gx")),
        check_vma=False,
    )
```

```python
import functools
import math

import jax
import jax.numpy as jnp
from jax import lax
from jax.experimental import pallas as pl
from jax.experimental.pallas import tpu as pltpu
from jax.sharding import PartitionSpec as P

SUB = 4
HALO = 8
VMEM_OUT = 8 * 1024 * 1024
LANES = 128
MESH = pl.DeviceIdType.MESH

U, V, WX, WY, THICK, STRENGTH, COVERED, MOVING = range(8)
FIELDS = 8


def kernel(
    dims,
    weight_ref,
    ocean_hbm,
    vel_hbm,
    wind_hbm,
    thick_hbm,
    conc_hbm,
    ice_hbm,
    land_hbm,
    fields,
    stress,
    ocean,
    total,
    y_send,
    y_recv,
    y_send_scale,
    y_recv_scale,
    z_send,
    z_recv,
    z_send_scale,
    z_recv_scale,
    masks,
    surf,
    ns_field,
    ew_field,
    ns_surf,
    side_send,
    side_recv,
    corner_recv,
    ocean_sem,
    static_sem,
    y_sems,
    z_sems,
    ns_sems,
    ew_sems,
    surf_sems,
):
    secs, rows_g, cols_g, levels = dims
    held = ocean_hbm.shape[0]
    tile_rows, tile_cols = thick_hbm.shape
    tiles = tile_cols // LANES
    top = 2 * HALO
    end = top + tile_rows
    s, g, x = lax.axis_index("sec"), lax.axis_index("gy"), lax.axis_index("gx")
    ranks = secs * rows_g
    rank = s * rows_g + g

    def at_rank(number):
        number = lax.rem(number + ranks, ranks)
        return (number // rows_g, lax.rem(number, rows_g), x)

    north, south = at_rank(rank - 1), at_rank(rank + 1)
    west = (s, g, lax.rem(x + cols_g - 1, cols_g))
    east = (s, g, lax.rem(x + 1, cols_g))
    north_west, north_east = north[:2] + west[2:], north[:2] + east[2:]
    south_west, south_east = south[:2] + west[2:], south[:2] + east[2:]
    over_secs = [(lax.rem(s + i, secs), g, x) for i in range(1, secs)]
    over_rows = [(s, lax.rem(g + k, rows_g), x) for k in range(1, rows_g)]

    order = [rows_g // 2] + [k for k in range(1, rows_g) if k != rows_g // 2] + [0]

    barrier = pltpu.get_barrier_semaphore()
    partners = over_secs + over_rows + [north, south, west, east]
    partners += [north_west, north_east, south_west, south_east]
    for partner in partners:
        pl.semaphore_signal(barrier, inc=1, device_id=partner, device_id_type=MESH)

    def block_rows(sec, k):
        block = sec * rows_g + lax.rem(g + k, rows_g)
        return pl.ds(pl.multiple_of(block * tile_rows, tile_rows), tile_rows)

    ocean_copies = {}
    for i in list(range(1, secs)) + [0]:
        for k in order:
            at = block_rows(lax.rem(s + i, secs), k)
            copy = pltpu.make_async_copy(
                ocean_hbm.at[:, :, at, :], ocean.at[i * rows_g + k], ocean_sem.at[i * rows_g + k]
            )
            copy.start()
            ocean_copies[i, k] = copy
    static_copies = []
    for j in range(tiles):
        cols = pl.ds(j * LANES, LANES)
        rows = pl.ds(top, tile_rows)
        for n, (source, target) in enumerate(
            (
                (vel_hbm.at[:, :, cols], fields.at[pl.ds(U, 2), j, rows, :]),
                (wind_hbm.at[:, :, cols], fields.at[pl.ds(WX, 2), j, rows, :]),
                (thick_hbm.at[:, cols], fields.at[THICK, j, rows, :]),
                (conc_hbm.at[:, cols], fields.at[STRENGTH, j, rows, :]),
                (ice_hbm.at[:, cols], masks.at[0, j]),
                (land_hbm.at[:, cols], masks.at[1, j]),
            )
        ):
            copy = pltpu.make_async_copy(source, target, static_sem.at[j, n])
            copy.start()
            static_copies.append(copy)

    def remote(source, target, sems, device):
        return pltpu.make_async_remote_copy(
            src_ref=source,
            dst_ref=target,
            send_sem=sems.at[0],
            recv_sem=sems.at[1],
            device_id=device,
            device_id_type=MESH,
        )

    own_weights = [weight_ref[rank * held + k] for k in range(held)]
    strips = tile_rows // 16

    def level_sum(slot, c, at, j):
        cols = pl.ds(j * LANES, LANES)
        c = (c + 2) % 3
        value = own_weights[0] * ocean[slot, 0, c, at, cols].astype(jnp.float32)
        for k in range(1, held):
            value = value + own_weights[k] * ocean[slot, k, c, at, cols].astype(jnp.float32)
        return value

    def twice(value):
        return jnp.concatenate([value, value], axis=0)

    def coded(value_of, target, scale_ref):
        def first(i, most):
            at = pl.ds(pl.multiple_of(i * 16, 16), 16)
            for j in range(tiles):
                value = value_of(at, j)
                total[at, pl.ds(j * LANES, LANES)] = value
                most = jnp.maximum(most, jnp.abs(value))
            return most

        most = lax.fori_loop(
            0, strips, first, jnp.zeros((16, LANES), jnp.float32), unroll=True
        )
        most = jnp.maximum(jnp.maximum(most[0:8], most[8:16]), 1e-30)
        scale_ref[...] = most * (1.0 / 32767.0)
        inverse = twice(32767.0 / most)

        @pl.loop(0, strips, unroll=True)
        def _(i):
            at = pl.ds(pl.multiple_of(i * 16, 16), 16)
            for j in range(tiles):
                cols = pl.ds(j * LANES, LANES)
                code = jnp.round(total[at, cols] * inverse)
                target[at, cols] = code.astype(jnp.int32).astype(jnp.int16)

    def decoded(code_ref, scale, at, j):
        code = code_ref[at, pl.ds(j * LANES, LANES)].astype(jnp.int32)
        return code.astype(jnp.float32) * scale

    y_copies = {}
    for i in range(1, secs):
        for k in order:
            ocean_copies[i, k].wait()
            for c in range(3):
                slot = ((i - 1) * rows_g + k, c)
                coded(
                    lambda at, j, i=i, k=k, c=c: level_sum(i * rows_g + k, c, at, j),
                    y_send.at[slot],
                    y_send_scale.at[slot],
                )
                if not y_copies:
                    pl.semaphore_wait(barrier, len(partners))
                pair = (
                    remote(y_send.at[slot], y_recv.at[slot], y_sems.at[slot + (0,)], over_secs[i - 1]),
                    remote(
                        y_send_scale.at[slot],
                        y_recv_scale.at[slot],
                        y_sems.at[slot + (1,)],
                        over_secs[i - 1],
                    ),
                )
                for copy in pair:
                    copy.start()
                y_copies[i, k, c] = pair

    for copy in static_copies:
        copy.wait()

    @pl.loop(0, tile_rows // 8)
    def _(i):
        at = pl.ds(pl.multiple_of(i * 8, 8), 8)
        to = pl.ds(pl.multiple_of(i * 8 + top, 8), 8)
        for j in range(tiles):
            conc = fields[STRENGTH, j, to, :]
            fields[STRENGTH, j, to, :] = jnp.exp(-4.0 * (1.0 - conc)) * fields[THICK, j, to, :]
            ice = masks[0, j, at, :].astype(jnp.float32)
            fields[COVERED, j, to, :] = ice
            fields[MOVING, j, to, :] = ice * masks[1, j, at, :].astype(jnp.float32)

    inner = pl.ds(0, tiles)

    def send_rows(source, target, sems):
        up = remote(
            source.at[:, inner, pl.ds(top, HALO), :], target.at[1], sems.at[0], north
        )
        down = remote(
            source.at[:, inner, pl.ds(end - HALO, HALO), :], target.at[0], sems.at[1], south
        )
        up.start()
        down.start()
        return up, down

    def place_rows(target, received, count):
        above = jnp.where(rank > 0, 1.0, 0.0)
        below = jnp.where(rank < ranks - 1, 1.0, 0.0)
        for f in range(count):
            for j in range(tiles):
                target[f, j, pl.ds(HALO, HALO), :] = received[0, f, j] * above
                target[f, j, pl.ds(end, HALO), :] = received[1, f, j] * below

    full = pl.ds(HALO, tile_rows + 2 * HALO)

    def send_columns(source, target, sems):
        left = remote(source.at[:, 0, full, :], target.at[1], sems.at[0], west)
        right = remote(source.at[:, tiles - 1, full, :], target.at[0], sems.at[1], east)
        left.start()
        right.start()
        return left, right

    lane = lax.broadcasted_iota(jnp.int32, (8, LANES), 1)
    all_strips = (tile_rows + 2 * HALO) // 8

    def place_columns(target, received, count):
        @pl.loop(0, all_strips)
        def _(i):
            at = pl.ds(pl.multiple_of(i * 8, 8), 8)
            to = pl.ds(pl.multiple_of(i * 8 + HALO, 8), 8)
            for f in range(count):
                target[f, tiles, to, :] = jnp.where(
                    lane < HALO,
                    received[1, f, at, :],
                    jnp.where(lane >= LANES - HALO, received[0, f, at, :], 0.0),
                )

    field_rows = send_rows(fields, ns_field, ns_sems)

    every = tiles + 1

    def margins(target, count):
        zero = jnp.zeros((8, LANES), jnp.float32)
        for f in range(count):
            for j in range(every):
                target[f, j, pl.ds(0, HALO), :] = zero
                target[f, j, pl.ds(end + HALO, HALO), :] = zero

    def sides(values):
        before = [pltpu.roll(value, 1, 1) for value in values]
        after = [pltpu.roll(value, LANES - 1, 1) for value in values]
        out = []
        for j in range(every):
            low = jnp.where(lane == 0, before[j - 1], before[j])
            high = jnp.where(lane == LANES - 1, after[(j + 1) % every], after[j])
            out.append(0.5 * (high - low))
        return out

    def strip_rows(i, shift):
        if shift == 0:
            return pl.ds(pl.multiple_of(i * 8 + HALO, 8), 8)
        return pl.ds(i * 8 + HALO + shift, 8)

    def rows_of(ref, f, at):
        return [ref[f, j, at, :] for j in range(every)]

    def stress_step(first):
        @pl.loop(0, all_strips, unroll=True)
        def _(i):
            at, up, down = strip_rows(i, 0), strip_rows(i, -1), strip_rows(i, 1)
            east_u = sides(rows_of(fields, U, at))
            east_v = sides(rows_of(fields, V, at))
            for j in range(every):
                north_u = 0.5 * (fields[U, j, down, :] - fields[U, j, up, :])
                north_v = 0.5 * (fields[V, j, down, :] - fields[V, j, up, :])
                spread = east_u[j] + north_v
                tension = east_u[j] - north_v
                shear = north_u + east_v[j]
                turned = lax.rsqrt(
                    spread * spread + 0.25 * (tension * tension + shear * shear) + 0.01
                )
                half = 0.5 * fields[STRENGTH, j, at, :]
                rate = half * turned
                covered = fields[COVERED, j, at, :] * (1.0 / 1.5)
                new0 = rate * spread - half
                new1 = (0.25 * rate) * tension
                new2 = (0.125 * rate) * shear
                if not first:
                    new0 = stress[0, j, at, :] + new0
                    new1 = stress[1, j, at, :] + new1
                    new2 = stress[2, j, at, :] + new2
                stress[0, j, at, :] = new0 * covered
                stress[1, j, at, :] = new1 * covered
                stress[2, j, at, :] = new2 * covered

    def velocity_step(first_strip=0, last_strip=all_strips, width=tiles + 1):
        @pl.loop(first_strip, last_strip, unroll=True)
        def _(i):
            at, up, down = strip_rows(i, 0), strip_rows(i, -1), strip_rows(i, 1)
            first = rows_of(stress, 0, at)
            second = rows_of(stress, 1, at)
            east_normal = sides([0.5 * (a + b) for a, b in zip(first, second)])
            east_third = sides(rows_of(stress, 2, at))
            for j in range(width):
                north_third = 0.5 * (stress[2, j, down, :] - stress[2, j, up, :])
                north_normal = 0.25 * (
                    (stress[0, j, down, :] - stress[1, j, down, :])
                    - (stress[0, j, up, :] - stress[1, j, up, :])
                )
                u, v = fields[U, j, at, :], fields[V, j, at, :]
                cx, cy = surf[1, j, at, :], surf[2, j, at, :]
                mass = fields[THICK, j, at, :]
                rel_u, rel_v = cx - u, cy - v
                drag = 0.8 * jnp.sqrt(rel_u * rel_u + rel_v * rel_v)
                a = mass + drag
                b = 0.5 * mass
                rx = mass * u + (east_normal[j] + north_third) + drag * cx + fields[WX, j, at, :]
                ry = mass * v + (east_third[j] + north_normal) + drag * cy + fields[WY, j, at, :]
                live = fields[MOVING, j, at, :] > 0.5
                inverse = 1.0 / jnp.where(live, a * a + b * b, 1.0)
                fields[U, j, at, :] = jnp.where(live, (a * rx + b * ry) * inverse, 0.0)
                fields[V, j, at, :] = jnp.where(live, (a * ry - b * rx) * inverse, 0.0)

    norm = 1.0 / math.sqrt(levels)
    tile_strips = tile_rows // 8
    per_piece = LANES // HALO
    halo_copies = []
    def surface_of(c, value_of):
        for k in range(rows_g - 1):
            for copy in z_copies[k * 3 + c]:
                copy.wait_recv()
        scales = [twice(z_recv_scale[k, c]) for k in range(rows_g - 1)]

        @pl.loop(0, strips, unroll=True)
        def _(i):
            at = pl.ds(pl.multiple_of(i * 16, 16), 16)
            to = pl.ds(pl.multiple_of(i * 16 + top, 8), 16)
            for j in range(tiles):
                value = value_of(at, j)
                for k in range(rows_g - 1):
                    value = value + decoded(z_recv.at[k, c], scales[k], at, j)
                surf[c, j, to, :] = value * norm

        for side, j, offset in ((0, 0, 0), (1, tiles - 1, HALO)):
            for piece in range(-(-tile_strips // per_piece)):
                packed = jnp.zeros((8, LANES), jnp.float32)
                for q in range(min(per_piece, tile_strips - piece * per_piece)):
                    value = surf[c, j, pl.ds(top + 8 * (piece * per_piece + q), 8), :]
                    shift = (q * HALO + offset) % LANES
                    value = pltpu.roll(value, shift, 1) if shift else value
                    packed = jnp.where(lane // HALO == q, value, packed)
                side_send[c, side, piece] = packed
        first, last = pl.ds(top, HALO), pl.ds(end - HALO, HALO)
        copies = []
        for n, (source, target, device) in enumerate(
            (
                (surf.at[c, inner, first, :], ns_surf.at[1, c], north),
                (surf.at[c, inner, last, :], ns_surf.at[0, c], south),
                (side_send.at[c, 0], side_recv.at[c, 1], west),
                (side_send.at[c, 1], side_recv.at[c, 0], east),
                (surf.at[c, 0, first, :], corner_recv.at[c, 3], north_west),
                (surf.at[c, tiles - 1, first, :], corner_recv.at[c, 2], north_east),
                (surf.at[c, 0, last, :], corner_recv.at[c, 1], south_west),
                (surf.at[c, tiles - 1, last, :], corner_recv.at[c, 0], south_east),
            )
        ):
            copy = remote(source, target, surf_sems.at[c, n], device)
            copy.start()
            copies.append(copy)
        halo_copies.append(copies)

    z_copies = []
    field_columns = None
    for k in order:
        ocean_copies[0, k].wait()
        for c in range(3):
            slots = [((i - 1) * rows_g + k, c) for i in range(1, secs)]
            for i in range(1, secs):
                for copy in y_copies[i, k, c]:
                    copy.wait_recv()
            scales = [twice(y_recv_scale[slot]) for slot in slots]

            def value_of(at, j, k=k, c=c, slots=slots, scales=scales):
                value = level_sum(k, c, at, j)
                for slot, scale in zip(slots, scales):
                    value = value + decoded(y_recv.at[slot], scale, at, j)
                return value

            if k == 0:
                surface_of(c, value_of)
                if c == 0:
                    for copy in field_columns:
                        copy.wait()
                    place_columns(fields, ew_field, FIELDS)
                    margins(fields, 2)
                    margins(stress, 3)
                    margins(surf, 3)
                    stress_step(True)
            else:
                slot = (k - 1, c)
                coded(value_of, z_send.at[slot], z_send_scale.at[slot])
                pair = (
                    remote(z_send.at[slot], z_recv.at[slot], z_sems.at[slot + (0,)], over_rows[k - 1]),
                    remote(
                        z_send_scale.at[slot],
                        z_recv_scale.at[slot],
                        z_sems.at[slot + (1,)],
                        over_rows[k - 1],
                    ),
                )
                for copy in pair:
                    copy.start()
                z_copies.append(pair)
        if k == order[0]:
            for copy in field_rows:
                copy.wait()
            place_rows(fields, ns_field, FIELDS)
            field_columns = send_columns(fields, ew_field, ew_sems)

    above = jnp.where(rank > 0, 1.0, 0.0)
    below = jnp.where(rank < ranks - 1, 1.0, 0.0)
    for c in range(3):
        for copy in halo_copies[c]:
            copy.wait()
        for j in range(tiles):
            surf[c, j, pl.ds(HALO, HALO), :] = ns_surf[0, c, j] * above
            surf[c, j, pl.ds(end, HALO), :] = ns_surf[1, c, j] * below

        def beyond(west_value, east_value):
            return jnp.where(
                lane < HALO, east_value, jnp.where(lane >= LANES - HALO, west_value, 0.0)
            )

        surf[c, tiles, pl.ds(HALO, HALO), :] = above * beyond(corner_recv[c, 0], corner_recv[c, 1])
        surf[c, tiles, pl.ds(end, HALO), :] = below * beyond(corner_recv[c, 2], corner_recv[c, 3])
        for t in range(tile_strips):
            piece, q = divmod(t, per_piece)
            from_west = side_recv[c, 0, piece]
            from_east = side_recv[c, 1, piece]
            back = (LANES - HALO - q * HALO) % LANES
            from_west = pltpu.roll(from_west, back, 1) if back else from_west
            back = (LANES - q * HALO) % LANES
            from_east = pltpu.roll(from_east, back, 1) if back else from_east
            surf[c, tiles, pl.ds(top + 8 * t, 8), :] = beyond(from_west, from_east)
        if c == 0:

            @pl.loop(0, all_strips, unroll=True)
            def _(i):
                at, up, down = strip_rows(i, 0), strip_rows(i, -1), strip_rows(i, 1)
                slope_x = sides(rows_of(surf, 0, at))
                for j in range(every):
                    slope_y = 0.5 * (surf[0, j, down, :] - surf[0, j, up, :])
                    gain = -0.5 * fields[THICK, j, at, :]
                    fields[WX, j, at, :] = fields[WX, j, at, :] + gain * slope_x[j]
                    fields[WY, j, at, :] = fields[WY, j, at, :] + gain * slope_y

    velocity_step()

    @pl.loop(0, SUB - 2)
    def _(cycle):
        stress_step(False)
        velocity_step()

    stress_step(False)
    velocity_step(1, all_strips - 1, tiles)
    for pair in list(y_copies.values()) + z_copies:
        for copy in pair:
            copy.wait_send()


def write_out(fields, stress, vel_out, stress_out, sems):
    tiles = fields.shape[1] - 1
    rows = pl.ds(2 * HALO, vel_out.shape[1])
    copies = []
    for j in range(tiles):
        cols = pl.ds(j * LANES, LANES)
        for n, (source, target) in enumerate(
            ((fields.at[pl.ds(U, 2)], vel_out), (stress, stress_out))
        ):
            copy = pltpu.make_async_copy(
                source.at[:, j, rows, :], target.at[:, :, cols], sems.at[n, j]
            )
            copy.start()
            copies.append(copy)
    for copy in copies:
        copy.wait()


def body(
    ocean, level_weight, velocity_start, wind_stress, thickness, concentration, ice_mask, land_mask
):
    secs, rows_g, cols_g = lax.axis_size("sec"), lax.axis_size("gy"), lax.axis_size("gx")
    held = ocean.shape[0]
    rows, cols = thickness.shape
    tiles = cols // LANES
    tall = rows + 4 * HALO
    wide_rows = rows + 2 * HALO
    pieces = pl.cdiv(rows, LANES)
    f32, i16 = jnp.float32, jnp.int16
    dma = pltpu.SemaphoreType.DMA
    y_slots = (secs - 1) * rows_g
    z_slots = rows_g - 1
    anywhere = pl.BlockSpec(memory_space=pl.ANY)
    on_chip = pl.BlockSpec(memory_space=pltpu.VMEM)
    fields, stress = pl.pallas_call(
        functools.partial(kernel, (secs, rows_g, cols_g, level_weight.shape[0])),
        out_shape=(
            pltpu.VMEM((FIELDS, tiles + 1, tall, LANES), f32),
            pltpu.VMEM((3, tiles + 1, tall, LANES), f32),
        ),
        in_specs=[pl.BlockSpec(memory_space=pltpu.SMEM)] + [anywhere] * 7,
        out_specs=(on_chip, on_chip),
        scratch_shapes=[
            pltpu.VMEM((secs * rows_g, held, 3, rows, cols), ocean.dtype),
            pltpu.VMEM((rows, cols), f32),
            pltpu.VMEM((y_slots, 3, rows, cols), i16),
            pltpu.VMEM((y_slots, 3, rows, cols), i16),
            pltpu.VMEM((y_slots, 3, 8, LANES), f32),
            pltpu.VMEM((y_slots, 3, 8, LANES), f32),
            pltpu.VMEM((z_slots, 3, rows, cols), i16),
            pltpu.VMEM((z_slots, 3, rows, cols), i16),
            pltpu.VMEM((z_slots, 3, 8, LANES), f32),
            pltpu.VMEM((z_slots, 3, 8, LANES), f32),
            pltpu.VMEM((2, tiles, rows, LANES), jnp.int32),
            pltpu.VMEM((3, tiles + 1, tall, LANES), f32),
            pltpu.VMEM((2, FIELDS, tiles, HALO, LANES), f32),
            pltpu.VMEM((2, FIELDS, wide_rows, LANES), f32),
            pltpu.VMEM((2, 3, tiles, HALO, LANES), f32),
            pltpu.VMEM((3, 2, pieces, 8, LANES), f32),
            pltpu.VMEM((3, 2, pieces, 8, LANES), f32),
            pltpu.VMEM((3, 4, HALO, LANES), f32),
            dma((secs * rows_g,)),
            dma((tiles, 6)),
            dma((y_slots, 3, 2, 2)),
            dma((z_slots, 3, 2, 2)),
            dma((2, 2)),
            dma((2, 2)),
            dma((3, 8, 2)),
        ],
        compiler_params=pltpu.CompilerParams(
            collective_id=0, has_side_effects=True, vmem_limit_bytes=52 * 1024 * 1024
        ),
    )(
        level_weight,
        ocean,
        velocity_start,
        wind_stress,
        thickness,
        concentration,
        ice_mask,
        land_mask,
    )
    return pl.pallas_call(
        write_out,
        out_shape=(
            jax.ShapeDtypeStruct((2, rows, cols), f32),
            jax.ShapeDtypeStruct((3, rows, cols), f32),
        ),
        in_specs=[on_chip, on_chip],
        out_specs=(anywhere, anywhere),
        scratch_shapes=[dma((2, tiles))],
        compiler_params=pltpu.CompilerParams(vmem_limit_bytes=VMEM_OUT),
    )(fields, stress)


def solution(mesh):
    placed = (
        P(("sec", "gy"), None, None, "gx"),
        P(),
        P(None, ("sec", "gy"), "gx"),
        P(None, ("sec", "gy"), "gx"),
        P(("sec", "gy"), "gx"),
        P(("sec", "gy"), "gx"),
        P(("sec", "gy"), "gx"),
        P(("sec", "gy"), "gx"),
    )
    return jax.shard_map(
        body,
        mesh=mesh,
        in_specs=placed,
        out_specs=(P(None, ("sec", "gy"), "gx"), P(None, ("sec", "gy"), "gx")),
        check_vma=False,
    )
```
